256 devices in a mesh: harm: 32 (over z, y_lo, core), space: 8 (over x, y_hi).
Axes of the slice: x: 4, y: 4 (y_hi: 2, y_lo: 2; y = y_hi * 2 + y_lo), z: 8, core: 2. Of those that a mesh axis runs over, the one named last changes fastest.
Arguments:
- forcing: float32 [32, 2, 4, 256, 1024], P('harm', None, None, 'space'), may hold values from -30 to 30
- coupling: bfloat16 [2, 2, 4, 4, 256, 1024], P(None, None, None, None, 'space'), may hold values from -1.5 to 1.5
- eddy: float32 [256, 1024], P('space'), may hold values from 0.1 to 1
- wake_mask: int32 [256, 1024], P('space'), may hold values 0 or 1
Outputs:
- solution: float32 [32, 2, 4, 256, 1024], P('harm', None, None, 'space')
- residual: float32 [32, 2, 4, 256, 1024], P('harm', None, None, 'space')
The draws below stay inside these ranges and needn't reach their ends.
All inputs are finite; a program needn't handle non-finite values. No bound on the sum of `wake_mask` on one device may be relied on, other than what follows from the above.
Results may differ from the reference program's by a relative error of at most 0.0003.
Values sent between devices are 32-bit elements; how exact they have to be, the bound alone decides.
No kernel may reach another device: no remote copies, remote signals or barrier semaphores. Data moves between devices by JAX's collectives and lax.ppermute only.
A program may use at most 64 MiB of HBM per device.

```python
import math
import jax
import jax.numpy as jnp
from jax import lax

NY = 1024
FIELDS = 4
HARMS = 32
NX = 256


def draw_forcing(key, part):
    key_base, key_cell = jax.random.split(key, 2)
    shape = (HARMS, 2, FIELDS, NX, NY)
    cell_scale = jnp.exp(jax.random.uniform(key_cell, (1, 1, 1, NX, NY), jnp.float32, jnp.log(0.3), jnp.log(3.0)))
    harm_pos = jnp.arange(HARMS).astype(jnp.float32)[:, None, None, None, None]
    row_pos = jnp.arange(NX).astype(jnp.float32)[None, None, None, :, None]
    amp = jnp.sqrt(1.0 + 2.0 * (harm_pos + row_pos / NX) / HARMS)
    base = jnp.clip(jax.random.normal(key_base, shape, jnp.float32), -5.0, 5.0)
    return (base * cell_scale * amp).astype(jnp.float32)


def touch_ends(array, rng, least, high):
    longest = array.shape.index(max(array.shape))
    spots = []
    for shift in (0, 1):
        where = [jax.random.randint(jax.random.fold_in(rng, axis), (), 0, length) for axis, length in enumerate(array.shape)]
        where[longest] = (where[longest] + shift) % array.shape[longest]
        spots.append(tuple(where))
    return array.at[spots[0]].set(least).at[spots[1]].set(high)


def level_of(stream_key, shape, cuts, smallest, top_value):
    def one(dim, shards_of):
        heights = jax.random.uniform(jax.random.fold_in(jax.random.fold_in(stream_key, 6), dim), (shards_of,), jnp.float32, smallest / len(cuts), top_value / len(cuts))
        return jnp.repeat(jnp.exp(heights), shape[dim] // shards_of).reshape((-1,) + (1,) * (len(shape) - dim - 1))

    gain = one(*cuts[0])
    for cut in cuts[1:]:
        gain = gain * one(*cut)
    return gain


def centred(stream_key, extent, width, reach, cuts=(), dtype=jnp.bfloat16):
    level = level_of(stream_key, extent, cuts, -0.22, 0.18) if cuts else 1.0
    array = jax.random.normal(stream_key, extent, jnp.float32) * width * level
    return jnp.minimum(jnp.maximum(array, -reach), reach).astype(dtype)


def setup_inputs(seed: int = 0) -> dict:
    splits = jax.random.split(jax.random.key(seed), 5)
    return {
        "forcing": draw_forcing(jax.random.fold_in(splits[4], 71), 0),
        "coupling": centred(splits[1], (2, 2, FIELDS, FIELDS, NX, NY), 0.25, 1.5, ((4, 8),)),
        "eddy": jnp.clip(jnp.exp(math.log(1.0) - 2.3025851 * jax.random.uniform(splits[2], (NX, NY), jnp.float32) ** level_of(splits[2], (NX, NY), ((0, 8),), -0.2, 0.2)), 0.1, 1.0),
        "wake_mask": touch_ends((jax.random.randint(splits[3], (NX, NY), 0, 2) < 1).astype(jnp.int32), jax.random.fold_in(splits[3], 1), 0, 1),
    }


sigma_shift = 1.0
omega_shed = 0.15
visc_floor = 0.05

def tmul(coef, state):
    return lax.optimization_barrier(jnp.sum(coef * state[..., :, None, :, :], axis=-4))

def couple(coef, state, hermitian):
    real_coef = coef[0].astype(jnp.float32)
    imag_coef = coef[1].astype(jnp.float32)
    real_part = state[..., 0, :, :, :]
    imag_part = state[..., 1, :, :, :]
    if hermitian:
        out_real = tmul(real_coef, real_part) + tmul(imag_coef, imag_part)
        out_imag = tmul(real_coef, imag_part) - tmul(imag_coef, real_part)
    else:
        out_real = tmul(real_coef, real_part) - tmul(imag_coef, imag_part)
        out_imag = tmul(real_coef, imag_part) + tmul(imag_coef, real_part)
    return jnp.stack([out_real, out_imag], axis=-4)

def apply_adjoint(state, coupling, visc):
    freq = (jnp.arange(HARMS) - HARMS // 2).astype(jnp.float32)
    phase = (omega_shed * freq)[:, None, None, None]
    real_part = state[:, 0]
    imag_part = state[:, 1]
    diag = jnp.stack([sigma_shift * real_part + phase * imag_part, sigma_shift * imag_part - phase * real_part], axis=1)
    scaled = visc * state
    padded = jnp.pad(scaled, ((0, 0), (0, 0), (0, 0), (1, 1), (1, 1)))
    neighbours = padded[..., 2:, 1:-1] + padded[..., :-2, 1:-1] + padded[..., 1:-1, 2:] + padded[..., 1:-1, :-2]
    diffused = 4.0 * scaled - neighbours
    zero_one = jnp.zeros_like(state[:1])
    zero_two = jnp.zeros_like(state[:2])
    after_one = jnp.concatenate([state[1:], zero_one], axis=0)
    after_two = jnp.concatenate([state[2:], zero_two], axis=0)
    before_one = jnp.concatenate([zero_one, state[:-1]], axis=0)
    before_two = jnp.concatenate([zero_two, state[:-2]], axis=0)
    first = coupling[0]
    second = coupling[1]
    triad = couple(first, after_one, True) + couple(second, after_two, True) + couple(first, before_one, False) + couple(second, before_two, False)
    return diag + diffused + triad

def reference(forcing, coupling, eddy, wake_mask):
    visc = visc_floor + wake_mask.astype(jnp.float32) * eddy
    beta = jnp.sqrt(jnp.sum(forcing * forcing))
    basis_one = forcing / beta
    image_one = apply_adjoint(basis_one, coupling, visc)
    h11 = jnp.sum(basis_one * image_one)
    remain_one = image_one - h11 * basis_one
    h21 = jnp.sqrt(jnp.sum(remain_one * remain_one))
    basis_two = remain_one / h21
    image_two = apply_adjoint(basis_two, coupling, visc)
    h12 = jnp.sum(basis_one * image_two)
    remain_two = image_two - h12 * basis_one
    h22 = jnp.sum(basis_two * remain_two)
    remain_three = remain_two - h22 * basis_two
    h32 = jnp.sqrt(jnp.sum(remain_three * remain_three))
    g11 = h11 * h11 + h21 * h21
    g12 = h11 * h12 + h21 * h22
    g22 = h12 * h12 + h22 * h22 + h32 * h32
    rhs_one = beta * h11
    rhs_two = beta * h12
    determ = g11 * g22 - g12 * g12
    coef_one = (g22 * rhs_one - g12 * rhs_two) / determ
    coef_two = (g11 * rhs_two - g12 * rhs_one) / determ
    solution = coef_one * basis_one + coef_two * basis_two
    residual = forcing - coef_one * image_one - coef_two * image_two
    return (solution, residual)
```

```python
import jax
import jax.numpy as jnp
from jax import lax
from jax.experimental import pallas as pl
from jax.experimental.pallas import tpu as pltpu
from jax.sharding import PartitionSpec as P

sigma_shift = 1.0
omega_shed = 0.15
visc_floor = 0.05

HARMS = 32
SPACE = 8
DEVICES = HARMS * SPACE
ROWS = 8
COLS = 1024
BLOCK = (8, ROWS, COLS)
F32 = jnp.float32


ANY = pl.BlockSpec(memory_space=pl.ANY)
VMEM = pl.BlockSpec(memory_space=pltpu.VMEM)


def shaped(*shape, dtype=F32):
    return jax.ShapeDtypeStruct(shape, dtype)


def params(mib=24):
    return pltpu.CompilerParams(vmem_limit_bytes=mib << 20)


def cost(flops, bytes_accessed):
    return pl.CostEstimate(flops=flops, bytes_accessed=bytes_accessed, transcendentals=0)


def place():
    harm = lax.axis_index("harm")
    return harm // 4, harm % 4


def swap(g, d):
    if d == 0:
        return g
    if d == 1:
        return g + 1 - 2 * (g % 2)
    if d == 2:
        return (g + 2) % 4
    return 3 - g


def eighth(q):
    return pl.ds(pl.multiple_of(q * ROWS, ROWS), ROWS)


def outer_slot(g, k):
    odd = (g + k) % 2
    upper = (g // 2 == 0) if k < 2 else (g // 2 == 1)
    return odd + jnp.where(upper, 6, 0)


def divide(x, y):
    good = y > 0.0
    return jnp.where(good, x / jnp.where(good, y, 1.0), 0.0)


def total(x):
    return jnp.sum(x, axis=(0, 1), keepdims=True)


def split_kernel(f_ref, o0, o1, o2, o3, sem):
    _, g = place()
    copies = [
        pltpu.make_async_copy(f_ref.at[:, eighth(swap(g, d)), :], out, sem.at[d])
        for d, out in enumerate((o0, o1, o2, o3))
    ]
    for copy in copies:
        copy.start()
    for copy in copies:
        copy.wait()


def split(f):
    return pl.pallas_call(
        split_kernel,
        out_shape=[shaped(*BLOCK)] * 4,
        in_specs=[ANY],
        out_specs=[VMEM] * 4,
        scratch_shapes=[pltpu.SemaphoreType.DMA((4,))],
        compiler_params=params(8),
        cost_estimate=cost(0, 2 << 20),
        name="split",
    )(f)


def local_kernel(c_ref, e_ref, m_ref, coef, visc, raw, eddy, mask, sem):
    _, g = place()
    copies = [
        pltpu.make_async_copy(c_ref.at[:, eighth(g), :], raw, sem.at[0]),
        pltpu.make_async_copy(e_ref.at[eighth(g), :], eddy, sem.at[1]),
        pltpu.make_async_copy(m_ref.at[eighth(g), :], mask, sem.at[2]),
    ]
    for copy in copies:
        copy.start()
    for copy in copies:
        copy.wait()
    visc[...] = visc_floor + mask[...].astype(F32) * eddy[...]

    def body(i, carry):
        coef[i] = raw[i].astype(F32)
        return carry

    lax.fori_loop(0, 64, body, 0)


def local_terms(coupling, eddy, mask):
    return pl.pallas_call(
        local_kernel,
        out_shape=[shaped(64, ROWS, COLS), shaped(ROWS, COLS)],
        in_specs=[ANY] * 3,
        out_specs=[VMEM] * 2,
        scratch_shapes=[
            pltpu.VMEM((64, ROWS, COLS), jnp.bfloat16),
            pltpu.VMEM((ROWS, COLS), F32),
            pltpu.VMEM((ROWS, COLS), jnp.int32),
            pltpu.SemaphoreType.DMA((3,)),
        ],
        compiler_params=params(8),
        cost_estimate=cost(1 << 20, 4 << 20),
        name="local_terms",
    )(coupling, eddy, mask)


def edge_kernel(b0, b1, b2, b3, visc, top, bottom):
    _, g = place()
    first = visc[0:1, :]
    last = visc[ROWS - 1 : ROWS, :]
    for d, block in enumerate((b0, b1, b2, b3)):
        j = swap(g, d)
        for c in range(8):
            top[j, c : c + 1, :] = first * block[c, 0:1, :]
            bottom[j, c : c + 1, :] = last * block[c, ROWS - 1 : ROWS, :]


def edges(blocks, visc):
    return pl.pallas_call(
        edge_kernel,
        out_shape=[shaped(4, 8, COLS)] * 2,
        in_specs=[VMEM] * 5,
        out_specs=[VMEM] * 2,
        compiler_params=params(8),
        cost_estimate=cost(1 << 16, 1 << 20),
        name="edges",
    )(*blocks, visc)


def spread(stage, acc, above, below, visc, z):
    v = visc[...]
    row = lax.broadcasted_iota(jnp.int32, (ROWS, COLS), 0)
    col = lax.broadcasted_iota(jnp.int32, (ROWS, COLS), 1)

    def neighbours(p, j, c):
        up = jnp.where(row == 0, above[j, c : c + 1, :], pltpu.roll(p, 1, 0))
        down = jnp.where(row == ROWS - 1, below[j, c : c + 1, :], pltpu.roll(p, ROWS - 1, 0))
        left = jnp.where(col == 0, 0.0, pltpu.roll(p, 1, 1))
        right = jnp.where(col == COLS - 1, 0.0, pltpu.roll(p, COLS - 1, 1))
        return (down + up) + (right + left)

    def body(j, carry):
        phase = omega_shed * (4 * z + j - HARMS // 2).astype(F32)
        for c in range(4):
            a = stage[2 + j, c]
            b = stage[2 + j, 4 + c]
            pa = v * a
            pb = v * b
            acc[j, c] = sigma_shift * a + phase * b + (4.0 * pa - neighbours(pa, j, c))
            acc[j, 4 + c] = sigma_shift * b - phase * a + (4.0 * pb - neighbours(pb, j, 4 + c))
        return carry

    lax.fori_loop(0, 4, body, 0)


def triads(stage, acc, coef, cols):
    for j in range(4):
        out = [acc[j, c, :, cols] for c in range(8)]
        for m in (1, 2):
            for k in range(4):
                a_next, a_prev = stage[2 + j + m, k, :, cols], stage[2 + j - m, k, :, cols]
                b_next, b_prev = stage[2 + j + m, 4 + k, :, cols], stage[2 + j - m, 4 + k, :, cols]
                a_sum, a_dif = a_next + a_prev, a_next - a_prev
                b_sum, b_dif = b_next + b_prev, b_next - b_prev
                for c in range(4):
                    re = coef[32 * (m - 1) + 4 * k + c, :, cols]
                    im = coef[32 * (m - 1) + 16 + 4 * k + c, :, cols]
                    out[c] = out[c] + (re * a_sum + im * b_dif)
                    out[4 + c] = out[4 + c] + (re * b_sum - im * a_dif)
        for c in range(8):
            acc[j, c, :, cols] = out[c]


def tile(t):
    return pl.ds(pl.multiple_of(t * 128, 128), 128)


def first_kernel(
    b0, b1, b2, b3, n0, n1, n2, n3, above, below, coef, visc,
    w01, w23, w1, w2, w3, top, bottom, stats,
    stage, acc, sem,
):
    z, g = place()
    inner = [
        pltpu.make_async_copy(ref, stage.at[2 + swap(g, d)], sem.at[d])
        for d, ref in enumerate((b0, b1, b2, b3))
    ]
    outer = [
        pltpu.make_async_copy(ref, stage.at[outer_slot(g, k)], sem.at[4 + k])
        for k, ref in enumerate((n0, n1, n2, n3))
    ]
    for copy in inner + outer:
        copy.start()
    for copy in inner:
        copy.wait()
    spread(stage, acc, above, below, visc, z)
    for copy in outer:
        copy.wait()

    def body(t, carry):
        ff, fw = carry
        cols = tile(t)
        triads(stage, acc, coef, cols)
        for j in range(4):
            for c in range(8):
                f = stage[2 + j, c, :, cols]
                ff = ff + f * f
                fw = fw + f * acc[j, c, :, cols]
        return ff, fw

    zero = jnp.zeros((ROWS, 128), F32)
    ff, fw = lax.fori_loop(0, COLS // 128, body, (zero, zero))
    s11, s12 = total(ff), total(fw)
    ratio = divide(s12, s11)

    def again(t, ww):
        cols = tile(t)
        for j in range(4):
            for c in range(8):
                w = acc[j, c, :, cols] - ratio * stage[2 + j, c, :, cols]
                ww = ww + w * w
        return ww

    s22 = total(lax.fori_loop(0, COLS // 128, again, zero))
    lane = lax.broadcasted_iota(jnp.int32, (8, 128), 1)
    stats[...] = jnp.where(lane == 0, s11, jnp.where(lane == 1, s12, jnp.where(lane == 2, s22, 0.0)))

    first = visc[0:1, :]
    last = visc[ROWS - 1 : ROWS, :]
    for j in range(4):
        for c in range(8):
            top[j, c : c + 1, :] = first * acc[j, c, 0:1, :]
            bottom[j, c : c + 1, :] = last * acc[j, c, ROWS - 1 : ROWS, :]
    w01[0] = acc[g]
    w01[1] = acc[swap(g, 1)]
    w23[0] = acc[swap(g, 2)]
    w23[1] = acc[swap(g, 3)]
    w1[...] = acc[swap(g, 1)]
    w2[...] = acc[swap(g, 2)]
    w3[...] = acc[swap(g, 3)]


def first_image(blocks, others, above, below, coef, visc):
    return pl.pallas_call(
        first_kernel,
        out_shape=[shaped(2, *BLOCK)] * 2
        + [shaped(*BLOCK)] * 3
        + [shaped(4, 8, COLS)] * 2
        + [shaped(8, 128)],
        in_specs=[ANY] * 8 + [VMEM] * 4,
        out_specs=[VMEM] * 8,
        scratch_shapes=[
            pltpu.VMEM((8, *BLOCK), F32),
            pltpu.VMEM((4, *BLOCK), F32),
            pltpu.SemaphoreType.DMA((8,)),
        ],
        compiler_params=params(24),
        cost_estimate=cost(50 << 20, 8 << 20),
        name="first_image",
    )(*blocks, *others, above, below, coef, visc)


def second_kernel(
    w01, w23, n01, n23, b0, b1, b2, b3, above, below, coef, visc, stats,
    z0, z1, z2, z3, factors,
    stage, base, acc, sem,
):
    z, g = place()
    inner = [
        pltpu.make_async_copy(ref, stage.at[2 + swap(g, d)], sem.at[d])
        for d, ref in enumerate((w01.at[0], w01.at[1], w23.at[0], w23.at[1]))
    ]
    outer = [
        pltpu.make_async_copy(ref, stage.at[outer_slot(g, k)], sem.at[4 + k])
        for k, ref in enumerate((n01.at[0], n01.at[1], n23.at[0], n23.at[1]))
    ]
    start = [
        pltpu.make_async_copy(ref, base.at[swap(g, d)], sem.at[8 + d])
        for d, ref in enumerate((b0, b1, b2, b3))
    ]
    for copy in inner + outer + start:
        copy.start()
    for copy in inner:
        copy.wait()
    spread(stage, acc, above, below, visc, z)
    for copy in outer + start:
        copy.wait()

    s11, s12, s22 = stats[0:1, 0:1], stats[0:1, 1:2], stats[0:1, 2:3]
    ratio = divide(s12, s11)

    def body(t, carry):
        fz, wz = carry
        cols = tile(t)
        triads(stage, acc, coef, cols)
        for j in range(4):
            for c in range(8):
                f = base[j, c, :, cols]
                w = stage[2 + j, c, :, cols] - ratio * f
                out = acc[j, c, :, cols]
                fz = fz + f * out
                wz = wz + w * out
        return fz, wz

    zero = jnp.zeros((ROWS, 128), F32)
    fz, wz = lax.fori_loop(0, COLS // 128, body, (zero, zero))
    s13, s23 = total(fz), total(wz)
    along_f = divide(s13, s11)
    along_w = divide(s23, s22)

    def again(t, zz):
        cols = tile(t)
        for j in range(4):
            for c in range(8):
                f = base[j, c, :, cols]
                w = stage[2 + j, c, :, cols] - ratio * f
                out = acc[j, c, :, cols] - along_f * f - along_w * w
                zz = zz + out * out
        return zz

    s33 = total(lax.fori_loop(0, COLS // 128, again, zero))
    a11, b22 = jnp.sqrt(s11), jnp.sqrt(s22)
    entries = (a11, ratio * a11, along_f * a11, b22, along_w * b22, jnp.sqrt(s33))
    lane = lax.broadcasted_iota(jnp.int32, (8, 128), 1)
    packed = jnp.zeros((8, 128), F32)
    for k, entry in enumerate(entries):
        packed = jnp.where(lane == k, entry, packed)
    for k in range(DEVICES // 8):
        factors[8 * k : 8 * k + 8, :] = packed
    z0[...] = acc[g]
    z1[...] = acc[swap(g, 1)]
    z2[...] = acc[swap(g, 2)]
    z3[...] = acc[swap(g, 3)]


def second_image(w01, w23, n01, n23, blocks, above, below, coef, visc, stats):
    return pl.pallas_call(
        second_kernel,
        out_shape=[shaped(*BLOCK)] * 4 + [shaped(DEVICES, 128)],
        in_specs=[ANY] * 8 + [VMEM] * 5,
        out_specs=[VMEM] * 5,
        scratch_shapes=[
            pltpu.VMEM((8, *BLOCK), F32),
            pltpu.VMEM((4, *BLOCK), F32),
            pltpu.VMEM((4, *BLOCK), F32),
            pltpu.SemaphoreType.DMA((12,)),
        ],
        compiler_params=params(24),
        cost_estimate=cost(50 << 20, 8 << 20),
        name="second_image",
    )(w01, w23, n01, n23, *blocks, above, below, coef, visc, stats)


def coefficients(factors):
    rows = jnp.transpose(factors)
    a11, a12, a13, b22, b23, c33 = [rows[k : k + 1, :] for k in range(6)]

    def add(x):
        return jnp.sum(x, axis=1, keepdims=True)

    beta_sq = add(a11 * a11)
    beta = jnp.sqrt(beta_sq)
    h11 = add(a11 * a12) / beta_sq
    t13 = add(a11 * a13) / beta_sq
    a12 = a12 - h11 * a11
    a13 = a13 - t13 * a11
    r22_sq = add(a12 * a12 + b22 * b22)
    r22 = jnp.sqrt(r22_sq)
    t23 = add(a12 * a13 + b22 * b23) / r22_sq
    a13 = a13 - t23 * a12
    b23 = b23 - t23 * b22
    r33 = jnp.sqrt(add(a13 * a13 + b23 * b23 + c33 * c33))
    h21 = r22 / beta
    h12 = (t13 - h11 * h11) / h21
    h22 = t23 - h11
    h32 = r33 / r22
    g11 = h11 * h11 + h21 * h21
    g12 = h11 * h12 + h21 * h22
    g22 = h12 * h12 + h22 * h22 + h32 * h32
    rhs_one = beta * h11
    rhs_two = beta * h12
    determ = g11 * g22 - g12 * g12
    coef_one = (g22 * rhs_one - g12 * rhs_two) / determ
    coef_two = (g11 * rhs_two - g12 * rhs_one) / determ
    return h11, coef_one / beta, coef_two / r22


def combine_kernel(
    f_ref, w01, w1, w2, w3, z0, z1, z2, z3, factors,
    sol_ref, res_ref,
    f, w, zz, sol, res, sem,
):
    _, g = place()
    loads = []
    for d, (wd, zd) in enumerate(((w01.at[0], z0), (w1, z1), (w2, z2), (w3, z3))):
        rows = eighth(swap(g, d))
        loads.append(
            (
                pltpu.make_async_copy(f_ref.at[:, rows, :], f.at[d], sem.at[0, d]),
                pltpu.make_async_copy(wd, w.at[d], sem.at[1, d]),
                pltpu.make_async_copy(zd, zz.at[d], sem.at[2, d]),
            )
        )
    for group in loads:
        for copy in group:
            copy.start()
    h11, one, two = coefficients(factors[...])
    stores = []
    for d, group in enumerate(loads):
        for copy in group:
            copy.wait()

        def body(c, carry, d=d):
            fv, wv, zv = f[d, c], w[d, c], zz[d, c]
            sol[d, c] = one * fv + two * (wv - h11 * fv)
            res[d, c] = fv - one * wv - two * (zv - h11 * wv)
            return carry

        lax.fori_loop(0, 8, body, 0)
        rows = eighth(swap(g, d))
        for source, target, k in ((sol, sol_ref, 3), (res, res_ref, 4)):
            copy = pltpu.make_async_copy(source.at[d], target.at[:, rows, :], sem.at[k, d])
            copy.start()
            stores.append(copy)
    for copy in stores:
        copy.wait()


def combine(f, w01, ws, zs, factors):
    return pl.pallas_call(
        combine_kernel,
        out_shape=[shaped(8, 4 * ROWS, COLS)] * 2,
        in_specs=[ANY] * 9 + [VMEM],
        out_specs=[ANY] * 2,
        scratch_shapes=[pltpu.VMEM((4, *BLOCK), F32)] * 5 + [pltpu.SemaphoreType.DMA((5, 4))],
        compiler_params=params(16),
        cost_estimate=cost(2 << 20, 5 << 20),
        name="combine",
    )(f, w01, *ws, *zs, factors)


def local(forcing, coupling, eddy, wake_mask):
    f = forcing.reshape(8, 4 * ROWS, COLS)

    def swapped(x, d):
        return lax.ppermute(x, "harm", [(h, h ^ d) for h in range(HARMS)])

    def along_z(x, outward, d=0):
        route = []
        for h in range(HARMS):
            up = (h % 4 >= 2) == outward
            target = h + 4 if up else h - 4
            if 0 <= target < HARMS:
                route.append((h, target ^ d))
        return lax.ppermute(x, "harm", route)

    def along_rows(x, step):
        route = []
        for h in range(HARMS):
            for s in range(SPACE):
                row = 4 * s + h % 4 + step
                if 0 <= row < 4 * SPACE:
                    target = (h - h % 4 + row % 4, row // 4)
                    route.append((h * SPACE + s, target[0] * SPACE + target[1]))
        return lax.ppermute(x, ("harm", "space"), route)

    own, part1, part2, part3 = split(f)
    from2 = swapped(part2, 2)
    from3 = swapped(part3, 3)
    from1 = swapped(part1, 1)
    near0 = along_z(own, True)
    near1 = along_z(part1, True, 1)
    far2 = along_z(from2, False)
    far3 = along_z(from3, False)
    coef, visc = local_terms(coupling.reshape(64, 4 * ROWS, COLS), eddy, wake_mask)
    blocks = (own, from1, from2, from3)
    top, bottom = edges(blocks, visc)
    above = along_rows(bottom, 1)
    below = along_rows(top, -1)
    w01, w23, w1, w2, w3, top, bottom, stats = first_image(
        blocks, (near0, near1, far2, far3), above, below, coef, visc
    )
    n01 = along_z(w01, True)
    n23 = along_z(w23, False)
    above = along_rows(bottom, 1)
    below = along_rows(top, -1)
    ws = [swapped(w2, 2), swapped(w3, 3), swapped(w1, 1)]
    z0, z1, z2, z3, factors = second_image(
        w01, w23, n01, n23, blocks, above, below, coef, visc, stats
    )
    zs = [swapped(z2, 2), swapped(z3, 3), swapped(z1, 1)]
    factors = lax.all_to_all(factors, ("harm", "space"), 0, 0, tiled=True)
    sol, res = combine(f, w01, (ws[2], ws[0], ws[1]), (z0, zs[2], zs[0], zs[1]), factors)
    return sol.reshape(forcing.shape), res.reshape(forcing.shape)


def solution(mesh):
    placed = (
        P("harm", None, None, "space", None),
        P(None, None, None, None, "space", None),
        P("space", None),
        P("space", None),
    )
    return jax.shard_map(
        local,
        mesh=mesh,
        in_specs=placed,
        out_specs=(P("harm", None, None, "space", None), P("harm", None, None, "space", None)),
        check_vma=False,
    )
```

```python
import jax
import jax.numpy as jnp
from jax import lax
from jax.experimental import pallas as pl
from jax.experimental.pallas import tpu as pltpu
from jax.sharding import PartitionSpec as P


sigma_shift = 1.0
omega_shed = 0.15
visc_floor = 0.05

HARMS = 32
SPACE = 8
DEVICES = HARMS * SPACE
ROWS = 8
COLS = 1024
BLOCK = (8, ROWS, COLS)
F32 = jnp.float32


ANY = pl.BlockSpec(memory_space=pl.ANY)
VMEM = pl.BlockSpec(memory_space=pltpu.VMEM)
HBM = pl.BlockSpec(memory_space=pltpu.HBM)


def shaped(*shape, dtype=F32):
    return jax.ShapeDtypeStruct(shape, dtype)


def params(mib=24):
    return pltpu.CompilerParams(vmem_limit_bytes=mib << 20)


def cost(flops, bytes_accessed):
    return pl.CostEstimate(flops=flops, bytes_accessed=bytes_accessed, transcendentals=0)


def place():
    harm = lax.axis_index("harm")
    return harm // 4, harm % 4


def swap(g, d):
    if d == 0:
        return g
    if d == 1:
        return g + 1 - 2 * (g % 2)
    if d == 2:
        return (g + 2) % 4
    return 3 - g


def eighth(q):
    return pl.ds(pl.multiple_of(q * ROWS, ROWS), ROWS)


def divide(x, y):
    good = y > 0.0
    return jnp.where(good, x / jnp.where(good, y, 1.0), 0.0)


def total(x):
    return jnp.sum(x, axis=(0, 1), keepdims=True)


def split_kernel(f_ref, o0, o1, o2, o3, sem):
    _, g = place()
    copies = [
        pltpu.make_async_copy(f_ref.at[:, eighth(swap(g, d)), :], out, sem.at[d])
        for d, out in enumerate((o0, o1, o2, o3))
    ]
    for copy in copies:
        copy.start()
    for copy in copies:
        copy.wait()


def split(f):
    return pl.pallas_call(
        split_kernel,
        out_shape=[shaped(*BLOCK)] * 4,
        in_specs=[HBM],
        out_specs=[VMEM] * 4,
        scratch_shapes=[pltpu.SemaphoreType.DMA((4,))],
        compiler_params=params(8),
        cost_estimate=cost(0, 2 << 20),
        name="split",
    )(f)


def local_kernel(c_ref, e_ref, m_ref, coef, visc, raw, eddy, mask, sem):
    _, g = place()
    copies = [
        pltpu.make_async_copy(c_ref.at[:, eighth(g), :], raw, sem.at[0]),
        pltpu.make_async_copy(e_ref.at[eighth(g), :], eddy, sem.at[1]),
        pltpu.make_async_copy(m_ref.at[eighth(g), :], mask, sem.at[2]),
    ]
    for copy in copies:
        copy.start()
    for copy in copies:
        copy.wait()
    visc[...] = visc_floor + mask[...].astype(F32) * eddy[...]

    def body(i, carry):
        coef[i] = raw[i].astype(F32)
        return carry

    lax.fori_loop(0, 64, body, 0)


def local_terms(coupling, eddy, mask):
    return pl.pallas_call(
        local_kernel,
        out_shape=[shaped(64, ROWS, COLS), shaped(ROWS, COLS)],
        in_specs=[HBM] * 3,
        out_specs=[VMEM] * 2,
        scratch_shapes=[
            pltpu.VMEM((64, ROWS, COLS), jnp.bfloat16),
            pltpu.VMEM((ROWS, COLS), F32),
            pltpu.VMEM((ROWS, COLS), jnp.int32),
            pltpu.SemaphoreType.DMA((3,)),
        ],
        compiler_params=params(8),
        cost_estimate=cost(1 << 20, 4 << 20),
        name="local_terms",
    )(coupling, eddy, mask)


def edge_kernel(b0, b1, b2, b3, visc, top, bottom):
    _, g = place()
    first = visc[0:1, :]
    last = visc[ROWS - 1 : ROWS, :]
    for d, block in enumerate((b0, b1, b2, b3)):
        j = swap(g, d)
        for c in range(8):
            top[j, c : c + 1, :] = first * block[c, 0:1, :]
            bottom[j, c : c + 1, :] = last * block[c, ROWS - 1 : ROWS, :]


def edge_pairs_kernel(p01, p23, visc, top, bottom):
    edge_kernel(p01.at[0], p01.at[1], p23.at[0], p23.at[1], visc, top, bottom)


def edges(blocks, visc):
    return pl.pallas_call(
        edge_kernel if len(blocks) == 4 else edge_pairs_kernel,
        out_shape=[shaped(4, 8, COLS)] * 2,
        in_specs=[VMEM] * (len(blocks) + 1),
        out_specs=[VMEM] * 2,
        compiler_params=params(8),
        cost_estimate=cost(1 << 16, 1 << 18),
        name="edges",
    )(*blocks, visc)


def tile(t):
    return pl.ds(pl.multiple_of(t * 128, 128), 128)


def spread(stage, acc, visc, z):
    v = visc[...]
    row = lax.broadcasted_iota(jnp.int32, (ROWS, COLS), 0)
    col = lax.broadcasted_iota(jnp.int32, (ROWS, COLS), 1)

    def neighbours(p):
        up = jnp.where(row == 0, 0.0, pltpu.roll(p, 1, 0))
        down = jnp.where(row == ROWS - 1, 0.0, pltpu.roll(p, ROWS - 1, 0))
        left = jnp.where(col == 0, 0.0, pltpu.roll(p, 1, 1))
        right = jnp.where(col == COLS - 1, 0.0, pltpu.roll(p, COLS - 1, 1))
        return (down + up) + (right + left)

    def body(j, carry):
        phase = omega_shed * (4 * z + j - HARMS // 2).astype(F32)
        for c in range(4):
            a = stage[j, c]
            b = stage[j, 4 + c]
            pa = v * a
            pb = v * b
            acc[j, c] = sigma_shift * a + phase * b + (4.0 * pa - neighbours(pa))
            acc[j, 4 + c] = sigma_shift * b - phase * a + (4.0 * pb - neighbours(pb))
        return carry

    lax.fori_loop(0, 4, body, 0)


def inner_triads(stage, acc, coef, cols):
    for j in range(4):
        out = [acc[j, c, :, cols] for c in range(8)]
        for m in (1, 2):
            for k in range(4):
                a_dif = b_dif = a_sum = b_sum = None
                if j + m < 4:
                    a_sum = a_dif = stage[j + m, k, :, cols]
                    b_sum = b_dif = stage[j + m, 4 + k, :, cols]
                if j - m >= 0:
                    a, b = stage[j - m, k, :, cols], stage[j - m, 4 + k, :, cols]
                    a_sum = a if a_sum is None else a_sum + a
                    b_sum = b if b_sum is None else b_sum + b
                    a_dif = -a if a_dif is None else a_dif - a
                    b_dif = -b if b_dif is None else b_dif - b
                for c in range(4):
                    re = coef[32 * (m - 1) + 4 * k + c, :, cols]
                    im = coef[32 * (m - 1) + 16 + 4 * k + c, :, cols]
                    out[c] = out[c] + (re * a_sum + im * b_dif)
                    out[4 + c] = out[4 + c] + (re * b_sum - im * a_dif)
        for c in range(8):
            acc[j, c, :, cols] = out[c]


def inner_body(blocks, coef, visc, acc, stage):
    z, g = place()
    for d, block in enumerate(blocks):
        stage[swap(g, d)] = block[...]
    spread(stage, acc, visc, z)

    def body(t, carry):
        inner_triads(stage, acc, coef, tile(t))
        return carry

    lax.fori_loop(0, COLS // 128, body, 0)


def inner_kernel(b0, b1, b2, b3, coef, visc, acc, stage):
    inner_body((b0, b1, b2, b3), coef, visc, acc, stage)


def inner_pairs_kernel(p01, p23, coef, visc, acc, stage):
    inner_body((p01.at[0], p01.at[1], p23.at[0], p23.at[1]), coef, visc, acc, stage)


def inner(blocks, coef, visc):
    return pl.pallas_call(
        inner_kernel if len(blocks) == 4 else inner_pairs_kernel,
        out_shape=shaped(4, *BLOCK),
        in_specs=[VMEM] * (len(blocks) + 2),
        out_specs=VMEM,
        scratch_shapes=[pltpu.VMEM((4, *BLOCK), F32)],
        compiler_params=params(12),
        cost_estimate=cost(40 << 20, 4 << 20),
        name="inner",
    )(*blocks, coef, visc)


def outer_body(acc, beyond, above, below, coef, out, pair):
    _, g = place()
    odd = g % 2
    upper = (g // 2 == 0) if pair == 1 else (g // 2 == 1)
    close = jnp.where(upper, odd, 1 - odd)
    away = 1 - close
    sign = jnp.where(upper, 1.0, -1.0)
    last = jnp.where(upper, 3, 0)
    inside = jnp.where(upper, 2, 1)
    row = lax.broadcasted_iota(jnp.int32, (ROWS, 128), 0)

    def body(t, carry):
        cols = tile(t)

        def begin(j, c):
            up = jnp.where(row == 0, above[j, c : c + 1, cols], 0.0)
            down = jnp.where(row == ROWS - 1, below[j, c : c + 1, cols], 0.0)
            return acc[j, c, :, cols] - (up + down)

        one = [begin(last, c) for c in range(8)]
        two = [begin(inside, c) for c in range(8)]
        for k in range(4):
            a, b = beyond[close, k, :, cols], beyond[close, 4 + k, :, cols]
            sa, sb = sign * a, sign * b
            a_away, b_away = beyond[away, k, :, cols], beyond[away, 4 + k, :, cols]
            sa_away, sb_away = sign * a_away, sign * b_away
            for c in range(4):
                re, im = coef[4 * k + c, :, cols], coef[16 + 4 * k + c, :, cols]
                one[c] = one[c] + (re * a + im * sb)
                one[4 + c] = one[4 + c] + (re * b - im * sa)
                re, im = coef[32 + 4 * k + c, :, cols], coef[48 + 4 * k + c, :, cols]
                one[c] = one[c] + (re * a_away + im * sb_away)
                one[4 + c] = one[4 + c] + (re * b_away - im * sa_away)
                two[c] = two[c] + (re * a + im * sb)
                two[4 + c] = two[4 + c] + (re * b - im * sa)
        for c in range(8):
            out[away, c, :, cols] = one[c]
            out[close, c, :, cols] = two[c]
        return carry

    lax.fori_loop(0, COLS // 128, body, 0)


def first_outer_kernel(pair, acc, n0, n1, above, below, coef, out, *rest):
    singles, beyond = rest[:-1], rest[-1]
    beyond[0] = n0[...]
    beyond[1] = n1[...]
    outer_body(acc, beyond, above, below, coef, out, pair)
    for k, single in enumerate(singles):
        single[...] = out[k + 2 - len(singles)]


def first_outer(pair, acc, beyond, above, below, coef):
    singles = 2 if pair else 1
    return pl.pallas_call(
        lambda *refs: first_outer_kernel(pair, *refs),
        out_shape=[shaped(2, *BLOCK)] + [shaped(*BLOCK)] * singles,
        in_specs=[VMEM] * 6,
        out_specs=[VMEM] * (1 + singles),
        scratch_shapes=[pltpu.VMEM((2, *BLOCK), F32)],
        compiler_params=params(8),
        cost_estimate=cost(16 << 20, 4 << 20),
        name="first_outer",
    )(acc, *beyond, above, below, coef)


def over_pair(step):
    def body(t, carry):
        cols = tile(t)
        for i in range(2):
            for c in range(8):
                carry = step(carry, i, c, cols)
        return carry

    return body


def first_stats_kernel(b0, b1, b2, b3, p01, p23, stats):
    zero = jnp.zeros((ROWS, 128), F32)
    lane = lax.broadcasted_iota(jnp.int32, (8, 128), 1)
    packed = jnp.zeros((8, 128), F32)
    for pair, (fs, w) in enumerate((((b0, b1), p01), ((b2, b3), p23))):

        def sums(carry, i, c, cols, fs=fs, w=w):
            f = fs[i][c, :, cols]
            return carry[0] + f * f, carry[1] + f * w[i, c, :, cols]

        ff, fw = lax.fori_loop(0, COLS // 128, over_pair(sums), (zero, zero))
        s11, s12 = total(ff), total(fw)
        ratio = divide(s12, s11)

        def rest(carry, i, c, cols, fs=fs, w=w, ratio=ratio):
            r = w[i, c, :, cols] - ratio * fs[i][c, :, cols]
            return carry + r * r

        s22 = total(lax.fori_loop(0, COLS // 128, over_pair(rest), zero))
        for k, value in enumerate((s11, ratio, s22)):
            packed = jnp.where(lane == 8 * pair + k, value, packed)
    stats[...] = packed


def first_stats(blocks, p01, p23):
    return pl.pallas_call(
        first_stats_kernel,
        out_shape=shaped(8, 128),
        in_specs=[VMEM] * 6,
        out_specs=VMEM,
        compiler_params=params(8),
        cost_estimate=cost(4 << 20, 2 << 20),
        name="first_stats",
    )(*blocks, p01, p23)


def second_outer_kernel(
    pair, acc, beyond, above, below, coef, f0, f1, w, stats, *rest
):
    if pair == 1:
        known, za, zb, factors, out = rest
    else:
        za, zb, factors, out = rest
    outer_body(acc, beyond, above, below, coef, out, pair)
    za[...] = out[0]
    zb[...] = out[1]
    zero = jnp.zeros((ROWS, 128), F32)
    s11, ratio, s22 = [stats[0:1, 8 * pair + k : 8 * pair + k + 1] for k in range(3)]
    fs = (f0, f1)

    def sums(carry, i, c, cols):
        f = fs[i][c, :, cols]
        o = out[i, c, :, cols]
        return carry[0] + f * o, carry[1] + (w[i, c, :, cols] - ratio * f) * o

    fz, wz = lax.fori_loop(0, COLS // 128, over_pair(sums), (zero, zero))
    along_f = divide(total(fz), s11)
    along_w = divide(total(wz), s22)

    def left(carry, i, c, cols):
        f = fs[i][c, :, cols]
        o = out[i, c, :, cols] - along_f * f - along_w * (w[i, c, :, cols] - ratio * f)
        return carry + o * o

    s33 = total(lax.fori_loop(0, COLS // 128, over_pair(left), zero))
    a11, b22 = jnp.sqrt(s11), jnp.sqrt(s22)
    entries = (a11, ratio * a11, along_f * a11, b22, along_w * b22, jnp.sqrt(s33))
    lane = lax.broadcasted_iota(jnp.int32, (8, 128), 1)
    packed = known[...] if pair == 1 else jnp.zeros((8, 128), F32)
    for k, entry in enumerate(entries):
        packed = jnp.where(lane == 8 * pair + k, entry, packed)
    for k in range(factors.shape[0] // 8):
        factors[8 * k : 8 * k + 8, :] = packed


def second_outer(pair, acc, beyond, above, below, coef, fs, w, stats, *known):
    return pl.pallas_call(
        lambda *refs: second_outer_kernel(pair, *refs),
        out_shape=[shaped(*BLOCK)] * 2 + [shaped(DEVICES if pair else 8, 128)],
        in_specs=[VMEM] * (9 + len(known)),
        out_specs=[VMEM] * 3,
        scratch_shapes=[pltpu.VMEM((2, *BLOCK), F32)],
        compiler_params=params(8),
        cost_estimate=cost(18 << 20, 4 << 20),
        name="second_outer",
    )(acc, beyond, above, below, coef, *fs, w, stats, *known)


def coefficients(factors):
    rows = jnp.transpose(factors)
    a11, a12, a13, b22, b23, c33 = [
        jnp.concatenate([rows[k : k + 1, :], rows[8 + k : 9 + k, :]], axis=1) for k in range(6)
    ]

    def add(x):
        return jnp.sum(x, axis=1, keepdims=True)

    beta_sq = add(a11 * a11)
    beta = jnp.sqrt(beta_sq)
    h11 = add(a11 * a12) / beta_sq
    t13 = add(a11 * a13) / beta_sq
    a12 = a12 - h11 * a11
    a13 = a13 - t13 * a11
    r22_sq = add(a12 * a12 + b22 * b22)
    r22 = jnp.sqrt(r22_sq)
    t23 = add(a12 * a13 + b22 * b23) / r22_sq
    a13 = a13 - t23 * a12
    b23 = b23 - t23 * b22
    r33 = jnp.sqrt(add(a13 * a13 + b23 * b23 + c33 * c33))
    h21 = r22 / beta
    h12 = (t13 - h11 * h11) / h21
    h22 = t23 - h11
    h32 = r33 / r22
    g11 = h11 * h11 + h21 * h21
    g12 = h11 * h12 + h21 * h22
    g22 = h12 * h12 + h22 * h22 + h32 * h32
    rhs_one = beta * h11
    rhs_two = beta * h12
    determ = g11 * g22 - g12 * g12
    coef_one = (g22 * rhs_one - g12 * rhs_two) / determ
    coef_two = (g11 * rhs_two - g12 * rhs_one) / determ
    return h11, coef_one / beta, coef_two / r22


def combine_kernel(
    f, w01, w1, w2, w3, z0, z1, z2, z3, factors,
    sol_ref, res_ref,
    sol, res, sem,
):
    _, g = place()
    h11, one, two = coefficients(factors[...])
    stores = []
    for d, (w, zz) in enumerate(((w01.at[0], z0), (w1, z1), (w2, z2), (w3, z3))):
        rows = eighth(swap(g, d))
        for c in range(8):
            fv, wv, zv = f[c, rows, :], w[c], zz[c]
            sol[d, c] = one * fv + two * (wv - h11 * fv)
            res[d, c] = fv - one * wv - two * (zv - h11 * wv)
        for source, target, k in ((sol, sol_ref, 0), (res, res_ref, 1)):
            copy = pltpu.make_async_copy(source.at[d], target.at[:, rows, :], sem.at[k, d])
            copy.start()
            stores.append(copy)
    for copy in stores:
        copy.wait()


def combine(f, w01, ws, zs, factors):
    return pl.pallas_call(
        combine_kernel,
        out_shape=[shaped(8, 4 * ROWS, COLS)] * 2,
        in_specs=[VMEM] * 10,
        out_specs=[HBM] * 2,
        scratch_shapes=[pltpu.VMEM((4, *BLOCK), F32)] * 2 + [pltpu.SemaphoreType.DMA((2, 4))],
        compiler_params=params(16),
        cost_estimate=cost(2 << 20, 5 << 20),
        name="combine",
    )(f, w01, *ws, *zs, factors)


def local(forcing, coupling, eddy, wake_mask):
    f = forcing.reshape(8, 4 * ROWS, COLS)

    def swapped(x, d):
        return lax.ppermute(x, "harm", [(h, h ^ d) for h in range(HARMS)])

    def along_z(x, outward, d=0):
        route = []
        for h in range(HARMS):
            up = (h % 4 >= 2) == outward
            target = h + 4 if up else h - 4
            if 0 <= target < HARMS:
                route.append((h, target ^ d))
        return lax.ppermute(x, "harm", route)

    def along_rows(x, step):
        route = []
        for h in range(HARMS):
            for s in range(SPACE):
                row = 4 * s + h % 4 + step
                if 0 <= row < 4 * SPACE:
                    target = (h - h % 4 + row % 4, row // 4)
                    route.append((h * SPACE + s, target[0] * SPACE + target[1]))
        return lax.ppermute(x, ("harm", "space"), route)

    own, part1, part2, part3 = split(f)
    from2 = swapped(part2, 2)
    from3 = swapped(part3, 3)
    near0 = along_z(own, True)
    near1 = along_z(part1, True, 1)
    from1 = swapped(part1, 1)
    coef, visc = local_terms(coupling.reshape(64, 4 * ROWS, COLS), eddy, wake_mask)
    from2, visc = lax.optimization_barrier((from2, visc))
    far2 = along_z(from2, False)
    far3 = along_z(from3, False)
    blocks = (own, from1, from2, from3)
    top, bottom = edges(blocks, visc)
    above = along_rows(bottom, 1)
    below = along_rows(top, -1)
    acc = inner(blocks, coef, visc)
    w23, w2, w3 = first_outer(1, acc, (near0, near1), above, below, coef)
    n23 = along_z(w23, False)
    w01, w1 = first_outer(0, acc, (far2, far3), above, below, coef)
    n01 = along_z(w01, True)
    top, bottom = edges((w01, w23), visc)
    above = along_rows(bottom, 1)
    below = along_rows(top, -1)
    w2, w3, w1 = swapped(w2, 2), swapped(w3, 3), swapped(w1, 1)
    stats = first_stats(blocks, w01, w23)
    acc = inner((w01, w23), coef, visc)
    z0, z1, known = second_outer(0, acc, n23, above, below, coef, blocks[:2], w01, stats)
    z1 = swapped(z1, 1)
    z2, z3, factors = second_outer(
        1, acc, n01, above, below, coef, blocks[2:], w23, stats, known
    )
    z2 = swapped(z2, 2)
    z3 = swapped(z3, 3)
    factors, w1, w2, w3, z1 = lax.optimization_barrier((factors, w1, w2, w3, z1))
    factors = lax.all_to_all(factors, ("harm", "space"), 0, 0, tiled=True)
    sol, res = combine(f, w01, (w1, w2, w3), (z0, z1, z2, z3), factors)
    return sol.reshape(forcing.shape), res.reshape(forcing.shape)


def solution(mesh):
    placed = (
        P("harm", None, None, "space", None),
        P(None, None, None, None, "space", None),
        P("space", None),
        P("space", None),
    )
    return jax.shard_map(
        local,
        mesh=mesh,
        in_specs=placed,
        out_specs=(P("harm", None, None, "space", None), P("harm", None, None, "space", None)),
        check_vma=False,
    )
```

```python
import jax
import jax.numpy as jnp
from jax import lax
from jax.experimental import pallas as pl
from jax.experimental.pallas import tpu as pltpu
from jax.sharding import PartitionSpec as P


sigma_shift = 1.0
omega_shed = 0.15
visc_floor = 0.05

HARMS = 32
SPACE = 8
DEVICES = HARMS * SPACE
ROWS = 8
COLS = 1024
BLOCK = (8, ROWS, COLS)
F32 = jnp.float32


ANY = pl.BlockSpec(memory_space=pl.ANY)
VMEM = pl.BlockSpec(memory_space=pltpu.VMEM)
HBM = pl.BlockSpec(memory_space=pltpu.HBM)


def shaped(*shape, dtype=F32):
    return jax.ShapeDtypeStruct(shape, dtype)


def params(mib=24):
    return pltpu.CompilerParams(vmem_limit_bytes=mib << 20)


def cost(flops, bytes_accessed):
    return pl.CostEstimate(flops=flops, bytes_accessed=bytes_accessed, transcendentals=0)


def place():
    harm = lax.axis_index("harm")
    return harm // 4, harm % 4


def swap(g, d):
    if d == 0:
        return g
    if d == 1:
        return g + 1 - 2 * (g % 2)
    if d == 2:
        return (g + 2) % 4
    return 3 - g


def eighth(q):
    return pl.ds(pl.multiple_of(q * ROWS, ROWS), ROWS)


def divide(x, y):
    good = y > 0.0
    return jnp.where(good, x / jnp.where(good, y, 1.0), 0.0)


def total(x):
    return jnp.sum(x, axis=(0, 1), keepdims=True)


def split_kernel(f_ref, o0, o1, o2, o3, sem):
    _, g = place()
    copies = [
        pltpu.make_async_copy(f_ref.at[:, eighth(swap(g, d)), :], out, sem.at[d])
        for d, out in enumerate((o0, o1, o2, o3))
    ]
    for copy in copies:
        copy.start()
    for copy in copies:
        copy.wait()


def split(f):
    return pl.pallas_call(
        split_kernel,
        out_shape=[shaped(*BLOCK)] * 4,
        in_specs=[HBM],
        out_specs=[VMEM] * 4,
        scratch_shapes=[pltpu.SemaphoreType.DMA((4,))],
        compiler_params=params(8),
        cost_estimate=cost(0, 2 << 20),
        name="split",
    )(f)


def join_kernel(a, b, out):
    out[0] = a[...]
    out[1] = b[...]


def join(a, b):
    return pl.pallas_call(
        join_kernel,
        out_shape=shaped(2, *BLOCK),
        in_specs=[VMEM] * 2,
        out_specs=VMEM,
        compiler_params=params(8),
        cost_estimate=cost(0, 1 << 20),
        name="join",
    )(a, b)


def local_kernel(c_ref, e_ref, m_ref, coef, visc, raw, eddy, mask, sem):
    _, g = place()
    copies = [
        pltpu.make_async_copy(c_ref.at[:, eighth(g), :], raw, sem.at[0]),
        pltpu.make_async_copy(e_ref.at[eighth(g), :], eddy, sem.at[1]),
        pltpu.make_async_copy(m_ref.at[eighth(g), :], mask, sem.at[2]),
    ]
    for copy in copies:
        copy.start()
    for copy in copies:
        copy.wait()
    visc[...] = visc_floor + mask[...].astype(F32) * eddy[...]

    def body(i, carry):
        coef[i] = raw[i].astype(F32)
        return carry

    lax.fori_loop(0, 64, body, 0)


def local_terms(coupling, eddy, mask):
    return pl.pallas_call(
        local_kernel,
        out_shape=[shaped(64, ROWS, COLS), shaped(ROWS, COLS)],
        in_specs=[HBM] * 3,
        out_specs=[VMEM] * 2,
        scratch_shapes=[
            pltpu.VMEM((64, ROWS, COLS), jnp.bfloat16),
            pltpu.VMEM((ROWS, COLS), F32),
            pltpu.VMEM((ROWS, COLS), jnp.int32),
            pltpu.SemaphoreType.DMA((3,)),
        ],
        compiler_params=params(8),
        cost_estimate=cost(1 << 20, 4 << 20),
        name="local_terms",
    )(coupling, eddy, mask)


def edge_kernel(b0, b1, b2, b3, visc, top, bottom):
    _, g = place()
    first = visc[0:1, :]
    last = visc[ROWS - 1 : ROWS, :]
    for d, block in enumerate((b0, b1, b2, b3)):
        j = swap(g, d)
        for c in range(8):
            top[j, c : c + 1, :] = first * block[c, 0:1, :]
            bottom[j, c : c + 1, :] = last * block[c, ROWS - 1 : ROWS, :]


def edge_pairs_kernel(p01, p23, visc, top, bottom):
    edge_kernel(p01.at[0], p01.at[1], p23.at[0], p23.at[1], visc, top, bottom)


def edges(blocks, visc):
    return pl.pallas_call(
        edge_kernel if len(blocks) == 4 else edge_pairs_kernel,
        out_shape=[shaped(4, 8, COLS)] * 2,
        in_specs=[VMEM] * (len(blocks) + 1),
        out_specs=[VMEM] * 2,
        compiler_params=params(8),
        cost_estimate=cost(1 << 16, 1 << 18),
        name="edges",
    )(*blocks, visc)


def tile(t):
    return pl.ds(pl.multiple_of(t * 128, 128), 128)


def spread(stage, acc, visc, z):
    v = visc[...]
    row = lax.broadcasted_iota(jnp.int32, (ROWS, COLS), 0)
    col = lax.broadcasted_iota(jnp.int32, (ROWS, COLS), 1)

    def neighbours(p):
        up = jnp.where(row == 0, 0.0, pltpu.roll(p, 1, 0))
        down = jnp.where(row == ROWS - 1, 0.0, pltpu.roll(p, ROWS - 1, 0))
        left = jnp.where(col == 0, 0.0, pltpu.roll(p, 1, 1))
        right = jnp.where(col == COLS - 1, 0.0, pltpu.roll(p, COLS - 1, 1))
        return (down + up) + (right + left)

    def body(j, carry):
        phase = omega_shed * (4 * z + j - HARMS // 2).astype(F32)
        for c in range(4):
            a = stage[j, c]
            b = stage[j, 4 + c]
            pa = v * a
            pb = v * b
            acc[j, c] = sigma_shift * a + phase * b + (4.0 * pa - neighbours(pa))
            acc[j, 4 + c] = sigma_shift * b - phase * a + (4.0 * pb - neighbours(pb))
        return carry

    lax.fori_loop(0, 4, body, 0)


def inner_triads(stage, acc, coef, cols):
    for j in range(4):
        out = [acc[j, c, :, cols] for c in range(8)]
        for m in (1, 2):
            for k in range(4):
                a_dif = b_dif = a_sum = b_sum = None
                if j + m < 4:
                    a_sum = a_dif = stage[j + m, k, :, cols]
                    b_sum = b_dif = stage[j + m, 4 + k, :, cols]
                if j - m >= 0:
                    a, b = stage[j - m, k, :, cols], stage[j - m, 4 + k, :, cols]
                    a_sum = a if a_sum is None else a_sum + a
                    b_sum = b if b_sum is None else b_sum + b
                    a_dif = -a if a_dif is None else a_dif - a
                    b_dif = -b if b_dif is None else b_dif - b
                for c in range(4):
                    re = coef[32 * (m - 1) + 4 * k + c, :, cols]
                    im = coef[32 * (m - 1) + 16 + 4 * k + c, :, cols]
                    out[c] = out[c] + (re * a_sum + im * b_dif)
                    out[4 + c] = out[4 + c] + (re * b_sum - im * a_dif)
        for c in range(8):
            acc[j, c, :, cols] = out[c]


def inner_body(blocks, coef, visc, acc, stage):
    z, g = place()
    for d, block in enumerate(blocks):
        stage[swap(g, d)] = block[...]
    spread(stage, acc, visc, z)

    def body(t, carry):
        inner_triads(stage, acc, coef, tile(t))
        return carry

    lax.fori_loop(0, COLS // 128, body, 0)


def inner_kernel(b0, b1, b2, b3, coef, visc, acc, stage):
    inner_body((b0, b1, b2, b3), coef, visc, acc, stage)


def inner_pairs_kernel(p01, p23, coef, visc, acc, stage):
    inner_body((p01.at[0], p01.at[1], p23.at[0], p23.at[1]), coef, visc, acc, stage)


def inner(blocks, coef, visc):
    return pl.pallas_call(
        inner_kernel if len(blocks) == 4 else inner_pairs_kernel,
        out_shape=shaped(4, *BLOCK),
        in_specs=[VMEM] * (len(blocks) + 2),
        out_specs=VMEM,
        scratch_shapes=[pltpu.VMEM((4, *BLOCK), F32)],
        compiler_params=params(12),
        cost_estimate=cost(40 << 20, 4 << 20),
        name="inner",
    )(*blocks, coef, visc)


def outer_body(acc, beyond, above, below, coef, out, pair, also=None, count=0):
    z, g = place()
    space = lax.axis_index("space")
    odd = g % 2
    upper = (g // 2 == 0) if pair == 1 else (g // 2 == 1)
    close = jnp.where(upper, odd, 1 - odd)
    away = 1 - close
    keep = jnp.where(z == jnp.where(upper, HARMS // 4 - 1, 0), 0.0, 1.0)
    sign = jnp.where(upper, keep, -keep)
    last = jnp.where(upper, 3, 0)
    inside = jnp.where(upper, 2, 1)
    row = lax.broadcasted_iota(jnp.int32, (ROWS, 128), 0)
    first_row = (row == 0) & ((space != 0) | (g != 0))
    last_row = (row == ROWS - 1) & ((space != SPACE - 1) | (g != 3))

    def body(t, carry):
        cols = tile(t)

        def begin(j, c):
            up = jnp.where(first_row, above[j, c : c + 1, cols], 0.0)
            down = jnp.where(last_row, below[j, c : c + 1, cols], 0.0)
            return acc[j, c, :, cols] - (up + down)

        one = [begin(last, c) for c in range(8)]
        two = [begin(inside, c) for c in range(8)]
        for k in range(4):
            a, b = beyond[close, k, :, cols], beyond[close, 4 + k, :, cols]
            sa, sb = sign * a, sign * b
            a, b = keep * a, keep * b
            a_away, b_away = beyond[away, k, :, cols], beyond[away, 4 + k, :, cols]
            sa_away, sb_away = sign * a_away, sign * b_away
            a_away, b_away = keep * a_away, keep * b_away
            for c in range(4):
                re, im = coef[4 * k + c, :, cols], coef[16 + 4 * k + c, :, cols]
                one[c] = one[c] + (re * a + im * sb)
                one[4 + c] = one[4 + c] + (re * b - im * sa)
                re, im = coef[32 + 4 * k + c, :, cols], coef[48 + 4 * k + c, :, cols]
                one[c] = one[c] + (re * a_away + im * sb_away)
                one[4 + c] = one[4 + c] + (re * b_away - im * sa_away)
                two[c] = two[c] + (re * a + im * sb)
                two[4 + c] = two[4 + c] + (re * b - im * sa)
        for c in range(8):
            out[away, c, :, cols] = one[c]
            out[close, c, :, cols] = two[c]
        if also is None:
            return carry
        terms = [also(i, c, cols, v[c]) for i, v in ((away, one), (close, two)) for c in range(8)]
        return tuple(carry[k] + tree([term[k] for term in terms]) for k in range(count))

    zero = jnp.zeros((ROWS, 128), F32)
    return lax.fori_loop(0, COLS // 128, body, (zero,) * count)


def tree(terms):
    while len(terms) > 1:
        terms = [sum(terms[i + 1 : i + 2], terms[i]) for i in range(0, len(terms), 2)]
    return terms[0]


def first_outer_kernel(pair, acc, *refs):
    if pair == 1:
        beyond, above, below, coef, out, one, two = refs
        outer_body(acc, beyond, above, below, coef, out, pair)
        one[...] = out[0]
        two[...] = out[1]
    else:
        n0, n1, above, below, coef, out, two, beyond = refs
        beyond[0] = n0[...]
        beyond[1] = n1[...]
        outer_body(acc, beyond, above, below, coef, out, pair)
        two[...] = out[1]


def first_outer(pair, acc, beyond, above, below, coef):
    return pl.pallas_call(
        lambda *refs: first_outer_kernel(pair, *refs),
        out_shape=[shaped(2, *BLOCK)] + [shaped(*BLOCK)] * (1 + pair),
        in_specs=[VMEM] * (4 + len(beyond)),
        out_specs=[VMEM] * (2 + pair),
        scratch_shapes=[] if pair else [pltpu.VMEM((2, *BLOCK), F32)],
        compiler_params=params(8),
        cost_estimate=cost(16 << 20, 4 << 20),
        name="first_outer",
    )(acc, *beyond, above, below, coef)


def over_pair(step, count):
    def body(t, carry):
        cols = tile(t)
        terms = [step(i, c, cols) for i in range(2) for c in range(8)]
        return tuple(carry[k] + tree([term[k] for term in terms]) for k in range(count))

    zero = jnp.zeros((ROWS, 128), F32)
    return [total(x) for x in lax.fori_loop(0, COLS // 128, body, (zero,) * count)]


def first_stats_kernel(b0, b1, b2, b3, p01, p23, stats):
    lane = lax.broadcasted_iota(jnp.int32, (8, 128), 1)
    packed = jnp.zeros((8, 128), F32)
    for pair, (fs, w) in enumerate((((b0, b1), p01), ((b2, b3), p23))):

        def sums(i, c, cols, fs=fs, w=w):
            f = fs[i][c, :, cols]
            return f * f, f * w[i, c, :, cols]

        s11, s12 = over_pair(sums, 2)
        ratio = divide(s12, s11)

        def rest(i, c, cols, fs=fs, w=w, ratio=ratio):
            r = w[i, c, :, cols] - ratio * fs[i][c, :, cols]
            return (r * r,)

        (s22,) = over_pair(rest, 1)
        a11, b22 = jnp.sqrt(s11), jnp.sqrt(s22)
        values = (a11, ratio * a11, ratio * ratio * s11, b22, ratio * s22)
        values += (ratio, divide(1.0, a11), divide(1.0, b22))
        for k, value in enumerate(values):
            packed = jnp.where(lane == 8 * pair + k, value, packed)
    stats[...] = packed


def first_stats(blocks, p01, p23):
    return pl.pallas_call(
        first_stats_kernel,
        out_shape=shaped(8, 128),
        in_specs=[VMEM] * 6,
        out_specs=VMEM,
        compiler_params=params(8),
        cost_estimate=cost(4 << 20, 2 << 20),
        name="first_stats",
    )(*blocks, p01, p23)


def second_outer_kernel(pair, acc, beyond, above, below, coef, f, w, stats, *rest):
    if pair == 1:
        known, za, zb, factors, out = rest
    else:
        za, zb, factors, out = rest
    known_f, known_w, ratio, over_a, over_b = [
        stats[0:1, 8 * pair + k : 8 * pair + k + 1] for k in (2, 4, 5, 6, 7)
    ]

    def sums(i, c, cols, o):
        fv, wv = f[i, c, :, cols], w[i, c, :, cols]
        y = o - ratio * wv
        return fv * y, (wv - ratio * fv) * y, y * y

    fy, wy, yy = outer_body(acc, beyond, above, below, coef, out, pair, sums, 3)
    za[...] = out[0]
    zb[...] = out[1]
    fy, wy, yy = total(fy), total(wy), total(yy)
    along_f, along_w = fy * over_a, wy * over_b
    rest_sq = jnp.maximum(yy - along_f * along_f - along_w * along_w, 0.0)
    a13 = along_f + known_f * over_a
    b23 = along_w + known_w * over_b
    lane = lax.broadcasted_iota(jnp.int32, (8, 128), 1)
    packed = stats[...] if pair == 0 else known[...]
    for k, entry in ((2, a13), (4, b23), (5, rest_sq)):
        packed = jnp.where(lane == 8 * pair + k, entry, packed)
    for k in range(factors.shape[0] // 8):
        factors[8 * k : 8 * k + 8, :] = packed


def second_outer(pair, acc, beyond, above, below, coef, f, w, stats, *known):
    return pl.pallas_call(
        lambda *refs: second_outer_kernel(pair, *refs),
        out_shape=[shaped(*BLOCK)] * 2 + [shaped(DEVICES if pair else 8, 128)],
        in_specs=[VMEM] * (8 + len(known)),
        out_specs=[VMEM] * 3,
        scratch_shapes=[pltpu.VMEM((2, *BLOCK), F32)],
        compiler_params=params(8),
        cost_estimate=cost(18 << 20, 4 << 20),
        name="second_outer",
    )(acc, beyond, above, below, coef, f, w, stats, *known)


def coefficients(factors):
    rows = jnp.transpose(factors)
    a11, a12, a13, b22, b23, c33_sq = [
        jnp.concatenate([rows[k : k + 1, :], rows[8 + k : 9 + k, :]], axis=1) for k in range(6)
    ]

    def add(x):
        return jnp.sum(x, axis=1, keepdims=True)

    beta_sq = add(a11 * a11)
    beta = jnp.sqrt(beta_sq)
    h11 = add(a11 * a12) / beta_sq
    t13 = add(a11 * a13) / beta_sq
    a12 = a12 - h11 * a11
    a13 = a13 - t13 * a11
    r22_sq = add(a12 * a12 + b22 * b22)
    r22 = jnp.sqrt(r22_sq)
    t23 = add(a12 * a13 + b22 * b23) / r22_sq
    a13 = a13 - t23 * a12
    b23 = b23 - t23 * b22
    r33 = jnp.sqrt(add(a13 * a13 + b23 * b23 + c33_sq))
    h21 = r22 / beta
    h12 = (t13 - h11 * h11) / h21
    h22 = t23 - h11
    h32 = r33 / r22
    g11 = h11 * h11 + h21 * h21
    g12 = h11 * h12 + h21 * h22
    g22 = h12 * h12 + h22 * h22 + h32 * h32
    rhs_one = beta * h11
    rhs_two = beta * h12
    determ = g11 * g22 - g12 * g12
    coef_one = (g22 * rhs_one - g12 * rhs_two) / determ
    coef_two = (g11 * rhs_two - g12 * rhs_one) / determ
    return h11, coef_one / beta, coef_two / r22


def combine_kernel(
    f, w01, w1, w2, w3, z0, z1, z2, z3, factors,
    sol_ref, res_ref,
    sol, res, sem,
):
    _, g = place()
    h11, one, two = coefficients(factors[...])
    stores = []
    for d, (w, zz) in enumerate(((w01.at[0], z0), (w1, z1), (w2, z2), (w3, z3))):
        rows = eighth(swap(g, d))
        for c in range(8):
            fv, wv, zv = f[c, rows, :], w[c], zz[c]
            sol[d, c] = one * fv + two * (wv - h11 * fv)
            res[d, c] = fv - one * wv - two * (zv - h11 * wv)
        for source, target, k in ((sol, sol_ref, 0), (res, res_ref, 1)):
            copy = pltpu.make_async_copy(source.at[d], target.at[:, rows, :], sem.at[k, d])
            copy.start()
            stores.append(copy)
    for copy in stores:
        copy.wait()


def combine(f, w01, ws, zs, factors):
    return pl.pallas_call(
        combine_kernel,
        out_shape=[shaped(8, 4 * ROWS, COLS)] * 2,
        in_specs=[VMEM] * 10,
        out_specs=[HBM] * 2,
        scratch_shapes=[pltpu.VMEM((4, *BLOCK), F32)] * 2 + [pltpu.SemaphoreType.DMA((2, 4))],
        compiler_params=params(16),
        cost_estimate=cost(2 << 20, 5 << 20),
        name="combine",
    )(f, w01, *ws, *zs, factors)


def local(forcing, coupling, eddy, wake_mask):
    f = forcing.reshape(8, 4 * ROWS, COLS)

    def send(x, axes, route):
        return lax.ppermute(x, axes, route)

    def swapped(x, d):
        return send(x, "harm", [(h, h ^ d) for h in range(HARMS)])

    def along_z(x, outward):
        steps = [4 if (h % 4 >= 2) == outward else -4 for h in range(HARMS)]
        return send(x, "harm", [(h, (h + steps[h]) % HARMS) for h in range(HARMS)])

    def along_rows(x, step):
        route = []
        for h in range(HARMS):
            for s in range(SPACE):
                row = (4 * s + h % 4 + step) % (4 * SPACE)
                target = (h - h % 4 + row % 4) * SPACE + row // 4
                route.append((h * SPACE + s, target))
        return send(x, ("harm", "space"), route)

    own, part1, part2, part3 = split(f)
    from2 = swapped(part2, 2)
    from3 = swapped(part3, 3)
    from1 = swapped(part1, 1)
    f01 = join(own, from1)
    near = along_z(f01, True)
    inputs = (coupling.reshape(64, 4 * ROWS, COLS), eddy, wake_mask)
    inputs = [pltpu.with_memory_space_constraint(x, pltpu.HBM) for x in inputs]
    coef, visc = local_terms(*inputs)
    from2, visc = lax.optimization_barrier((from2, visc))
    far2 = along_z(from2, False)
    far3 = along_z(from3, False)
    blocks = (own, from1, from2, from3)
    top, bottom = edges(blocks, visc)
    above = along_rows(bottom, 1)
    below = along_rows(top, -1)
    acc = inner(blocks, coef, visc)
    w23, w2, w3 = first_outer(1, acc, (near,), above, below, coef)
    n23 = along_z(w23, False)
    w01, w1 = first_outer(0, acc, (far2, far3), above, below, coef)
    n01 = along_z(w01, True)
    top, bottom = edges((w01, w23), visc)
    above = along_rows(bottom, 1)
    below = along_rows(top, -1)
    w2, w3, w1 = swapped(w2, 2), swapped(w3, 3), swapped(w1, 1)
    stats = first_stats(blocks, w01, w23)
    f23 = join(from2, from3)
    acc = inner((w01, w23), coef, visc)
    z0, z1, known = second_outer(0, acc, n23, above, below, coef, f01, w01, stats)
    z1 = swapped(z1, 1)
    z2, z3, factors = second_outer(1, acc, n01, above, below, coef, f23, w23, stats, known)
    z2, z3 = swapped(z2, 2), swapped(z3, 3)
    factors = lax.all_to_all(factors, ("harm", "space"), 0, 0, tiled=True)
    sol, res = combine(f, w01, (w1, w2, w3), (z0, z1, z2, z3), factors)
    return sol.reshape(forcing.shape), res.reshape(forcing.shape)


def solution(mesh):
    placed = (
        P("harm", None, None, "space", None),
        P(None, None, None, None, "space", None),
        P("space", None),
        P("space", None),
    )
    return jax.shard_map(
        local,
        mesh=mesh,
        in_specs=placed,
        out_specs=(P("harm", None, None, "space", None), P("harm", None, None, "space", None)),
        check_vma=False,
    )
```
